32 devices in a mesh: slab: 8 (over z, x), depth: 4 (over y, core).
Axes of the slice: x: 2, y: 2, z: 4, core: 2. Of those that a mesh axis runs over, the one named last changes fastest.
Arguments:
- right_side: float32 [3, 8, 8, 32, 256], P(None, None, 'slab', 'depth'), may hold values from -4 to 9
- smoother: float32 [3, 8, 32, 256], P(None, 'slab', 'depth'), may hold values from 0.1 to 1
- material: int32 [8, 32, 256], P('slab', 'depth'), may hold values from 0 to 15
- moduli: float32 [16], replicated, may hold values from 0.25 to 4
- element_matrix: float32 [24, 24], replicated, may hold values from -0.15 to 3, as said below
- coarse_inverse: float32 [24, 24], replicated, may hold values from -0.2 to 1.2, as said below
- surface_map: int32 [8, 256], P('slab'), may hold values from 0 to 2047, as said below
- line_of_sight: float32 [3, 8, 256], P(None, 'slab'), may hold values from -3 to 3
Outputs:
- residual: float32 [3, 8, 8, 32, 256], P(None, None, 'slab', 'depth')
- pixels: float32 [8, 2048], P('depth', 'slab')
The draws below stay inside these ranges and needn't reach their ends.
Inputs may be any that keep to these rules, and one draw needn't show every extreme that they name: `element_matrix`: symmetric. `coarse_inverse`: symmetric. `surface_map`: pixel p lies in tile p // 256. At most 64 surface nodes of one slab block lie in one tile, and some tile holds exactly 64 surface nodes of every slab block.
All inputs are finite; a program needn't handle non-finite values.
Results may differ from the reference program's by a relative error of at most 0.0003.
Values sent between devices are 32-bit elements; how exact they have to be, the bound alone decides.
No kernel may reach another device: no remote copies, remote signals or barrier semaphores. Data moves between devices by JAX's collectives and lax.ppermute only.
A program may use at most 64 MiB of HBM per device.

```python
import math
import jax
import jax.numpy as jnp
from jax import lax

SRC = 8
NMAT = 16
CX = 1
NY = 256
PIX = 256
NX = 8
NZ = 32
PIXELS = 2048
N_SLAB = 8


def draw_right_side(key, part):
    first_key, second_key = jax.random.split(jax.random.fold_in(key, 11))
    n_blocks = NX // CX
    blocks = jnp.arange(n_blocks, dtype=jnp.float32)
    rising = 1.0 + 2.0 * blocks / max(n_blocks - 1, 1)
    roughness = jax.random.truncated_normal(first_key, -4.0, 4.0, (3, SRC, NX, NZ, NY), jnp.float32)
    amplitude = jax.random.uniform(second_key, (3, SRC, n_blocks), jnp.float32, 0.5, 1.5)
    smooth_part = jnp.repeat(amplitude * rising, CX, axis=2)
    return roughness + smooth_part[:, :, :, None, None]


def draw_element_matrix(key, part):
    first_key, second_key = jax.random.split(jax.random.fold_in(key, 23))
    normal_part = jax.random.truncated_normal(first_key, -4.0, 4.0, (24, 24), jnp.float32) * 0.02
    margin = jax.random.uniform(second_key, (24,), jnp.float32, 0.05, 0.15)
    off_diag = 0.5 * (normal_part + normal_part.T) * (1.0 - jnp.eye(24, dtype=jnp.float32))
    diagonal_part = jnp.sum(jnp.abs(off_diag), axis=1) + margin
    return off_diag + jnp.diag(diagonal_part)


def draw_coarse_inverse(key, part):
    size_kc = 3 * (NX // CX)
    normal_part = jax.random.truncated_normal(jax.random.fold_in(key, 37), -4.0, 4.0, (size_kc, size_kc), jnp.float32)
    normal_part = normal_part * (0.2 / size_kc ** 0.5)
    return jnp.eye(size_kc, dtype=jnp.float32) + 0.5 * (normal_part + normal_part.T)


def draw_surface_map(key, part):
    n_blocks = NX // CX
    node_count = CX * NY
    capacity = 2 * node_count // n_blocks
    pair_count = n_blocks // 2
    full_pair = jax.random.randint(jax.random.fold_in(key, 7), (), 0, pair_count)

    def one_block(block_id):
        block_key = jax.random.fold_in(key, block_id + 100)
        first_key, second_key, third_key = jax.random.split(block_key, 3)
        counts = jax.random.randint(first_key, (pair_count,), 0, capacity + 1)
        counts = jnp.where(jnp.arange(pair_count, dtype=jnp.int32) == full_pair, capacity, counts)
        positions = jnp.arange(node_count, dtype=jnp.int32)
        pair_of = positions // capacity
        within = positions % capacity
        tile_owner = 2 * pair_of + (within >= counts[pair_of]).astype(jnp.int32)
        shuffle = jax.random.permutation(second_key, node_count)
        tile_owner = tile_owner[shuffle]
        pixel_local = jax.random.randint(third_key, (node_count,), 0, PIX)
        return (tile_owner * PIX + pixel_local).astype(jnp.int32)
    tables = jax.vmap(one_block)(jnp.arange(n_blocks, dtype=jnp.int32))
    return tables.reshape(NX, NY)


def set_ends(values, own_key, low, top_value):
    shape = values.shape
    place = [jax.random.randint(jax.random.fold_in(own_key, axis), (), 0, shape[axis]) for axis in range(len(shape))]
    values = values.at[tuple(place)].set(low)
    longest = shape.index(max(shape))
    place[longest] = (place[longest] + 1) % shape[longest]
    return values.at[tuple(place)].set(top_value)


def steps_of(own_key, dims, cuts, smallest, top_value):
    factor_of, own = 1.0, jax.random.fold_in(own_key, 6)
    for position, blocks in cuts:
        heights = jnp.exp(jax.random.uniform(jax.random.fold_in(own, position), (blocks,), jnp.float32, smallest / len(cuts), top_value / len(cuts)))
        factor_of = factor_of * jnp.repeat(heights, dims[position] // blocks).reshape([-1 if axis == position else 1 for axis in range(len(dims))])
    return factor_of


def centred(own_key, dims, scale, limit, shards=(), kind=jnp.bfloat16):
    level = steps_of(own_key, dims, shards, -0.22, 0.18) if shards else 1.0
    array = jax.random.normal(own_key, dims, jnp.float32) * scale * level
    return jnp.minimum(jnp.maximum(array, -limit), limit).astype(kind)


def setup_inputs(seed: int = 0) -> dict:
    splits = jax.random.split(jax.random.key(seed), 9)
    right_side = draw_right_side(jax.random.fold_in(splits[8], 71), 0)
    smoother = jnp.clip(jnp.exp(math.log(1.0) - 2.3025851 * jax.random.uniform(splits[1], (3, NX, NZ, NY), jnp.float32) ** steps_of(splits[1], (3, NX, NZ, NY), ((1, 8), (2, 4)), -0.2, 0.2)), 0.1, 1.0)
    material = set_ends(jax.random.randint(splits[2], (NX, NZ, NY), 0, NMAT), jax.random.fold_in(splits[2], 1), 0, NMAT - 1).astype(jnp.int32)
    moduli = jnp.clip(jnp.exp(jax.random.uniform(splits[3], (NMAT,), jnp.float32, math.log(0.25), math.log(4.0))), 0.25, 4.0)
    element_matrix = draw_element_matrix(jax.random.fold_in(splits[8], 71), 0)
    coarse_inverse = draw_coarse_inverse(jax.random.fold_in(splits[8], 71), 0)
    surface_map = draw_surface_map(jax.random.fold_in(splits[8], 71), 0)
    line_of_sight = centred(splits[7], (3, NX, NY), 0.6, 3.0, ((1, 8),), jnp.float32)
    return dict(right_side=right_side, smoother=smoother, material=material, moduli=moduli, element_matrix=element_matrix, coarse_inverse=coarse_inverse, surface_map=surface_map, line_of_sight=line_of_sight)


def stiffness(padded_field, padded_moduli, element_matrix):
    sources = padded_field.shape[1]
    span_x = padded_field.shape[2] - 1
    span_z = padded_field.shape[3] - 1
    span_y = padded_moduli.shape[2]
    corners = []
    for corner in range(8):
        along_x, along_z, along_y = corner // 4, (corner // 2) % 2, corner % 2
        corners.append(padded_field[:, :, along_x:along_x + span_x, along_z:along_z + span_z, along_y:along_y + span_y])
    stacked = jnp.stack(corners, 0).reshape(24, -1)
    forces = jnp.dot(element_matrix, stacked, precision=lax.Precision.HIGHEST, preferred_element_type=jnp.float32)
    forces = forces.reshape(8, 3, sources, span_x, span_z, span_y) * padded_moduli[1:, 1:, :]
    forces = jnp.pad(forces, ((0, 0), (0, 0), (0, 0), (0, 0), (0, 0), (0, 1)))
    summed = jnp.zeros((3, sources, span_x - 1, span_z - 1, span_y), jnp.float32)
    for corner in range(8):
        along_x, along_z, along_y = corner // 4, (corner // 2) % 2, corner % 2
        summed = summed + forces[corner, :, :, 1 - along_x:1 - along_x + span_x - 1, 1 - along_z:1 - along_z + span_z - 1, 1 - along_y:1 - along_y + span_y]
    return summed


def reference(right_side, smoother, material, moduli, element_matrix, coarse_inverse, surface_map, line_of_sight):
    modulus_field = moduli[material]
    block_sums = right_side.reshape(3, SRC, N_SLAB, CX * NZ * NY).sum(-1)
    coarse_mean = jnp.transpose(block_sums, (2, 0, 1)).reshape(3 * N_SLAB, SRC) / (CX * NZ * NY)
    correction = jnp.dot(coarse_inverse, coarse_mean, precision=lax.Precision.HIGHEST, preferred_element_type=jnp.float32)
    per_block = jnp.transpose(correction.reshape(N_SLAB, 3, SRC), (1, 2, 0))
    per_node = jnp.repeat(per_block, CX, axis=2)
    direction = smoother[:, None] * right_side + per_node[:, :, :, None, None]
    numerator = jnp.sum(right_side * direction, axis=(0, 2, 3, 4))
    padded = jnp.pad(direction, ((0, 0), (0, 0), (1, 1), (1, 1), (1, 0)))
    moduli_pad = jnp.pad(modulus_field, ((1, 1), (1, 1), (0, 0)))

    def block_apply(block_index):
        offset = (block_index * CX).astype(jnp.int32)
        field_blk = lax.dynamic_slice_in_dim(padded, offset, CX + 2, 2)
        moduli_blk = lax.dynamic_slice_in_dim(moduli_pad, offset, CX + 2, 0)
        return stiffness(field_blk, moduli_blk, element_matrix)

    applied = lax.map(block_apply, jnp.arange(N_SLAB, dtype=jnp.int32))
    applied = jnp.transpose(applied, (1, 2, 0, 3, 4, 5)).reshape(3, SRC, NX, NZ, NY)
    denominator = jnp.sum(direction * applied, axis=(0, 2, 3, 4))
    step_size = numerator / denominator
    residual = right_side - step_size[None, :, None, None, None] * applied
    surface = step_size[None, :, None, None] * direction[:, :, :, NZ - 1, :]
    projected = jnp.sum(line_of_sight[:, None] * surface, axis=0)
    pixels = jnp.zeros((SRC, PIXELS), jnp.float32).at[:, surface_map.reshape(-1)].add(projected.reshape(SRC, -1))
    return residual, pixels
```

```python
import jax
import jax.numpy as jnp
from jax import lax
from jax.experimental import pallas as pl
from jax.experimental.pallas import tpu as pltpu
from jax.sharding import PartitionSpec as P

PIX = 256
LANES = 128
F32 = jnp.float32
BF16 = jnp.bfloat16

AT_NUM = 24
AT_DEN = 32
AT_LOW = 40
AT_OWN = 64
AT_MOD = 88


def iota(shape, dim):
    return lax.broadcasted_iota(jnp.int32, shape, dim)


def dot(a, b):
    return lax.dot_general(
        a, b, (((1,), (0,)), ((), ())), precision=lax.Precision.HIGHEST, preferred_element_type=F32
    )


def dot_t(a, b):
    return lax.dot_general(
        a, b, (((1,), (1,)), ((), ())), precision=lax.Precision.HIGHEST, preferred_element_type=F32
    )


def dot_b(a, b):
    return lax.dot_general(a, b, (((1,), (0,)), ((), ())), preferred_element_type=F32)


def dot_bt(a, b):
    return lax.dot_general(a, b, (((1,), (1,)), ((), ())), preferred_element_type=F32)


def split2(x):
    high = x.astype(BF16)
    low = (x - high.astype(F32)).astype(BF16)
    return high, low


def split3(x):
    high = x.astype(BF16)
    rest = x - high.astype(F32)
    mid = rest.astype(BF16)
    low = (rest - mid.astype(F32)).astype(BF16)
    return high, mid, low


def onehot(mask):
    return jnp.where(mask, 1.0, 0.0)


def next_lane(x, lane):
    return jnp.where(lane == x.shape[1] - 1, 0.0, pltpu.roll(x, x.shape[1] - 1, 1))


def prev_lane(x, lane):
    return jnp.where(lane == 0, 0.0, pltpu.roll(x, 1, 1))


def to_halves(ref, halves):
    for h, half in enumerate(halves):
        half[...] = ref[:, h * LANES : (h + 1) * LANES]


def strided(halves, start, rows, stride):
    return jnp.concatenate([half[pl.ds(start, rows, stride=stride), :] for half in halves], 1)


def weigh_kernel(comps, srcs, wz, r_ref, s_ref, u_ref, top_ref, part_ref, *halves):
    rows = comps * srcs
    to_halves(r_ref, halves)
    acc_r = acc_ru = None
    for z in range(wz):
        force = strided(halves, z, rows, wz)
        weight = jnp.concatenate(
            [
                jnp.broadcast_to(s_ref[m * wz + z : m * wz + z + 1, :], (srcs, force.shape[1]))
                for m in range(comps)
            ],
            0,
        )
        u = force * weight
        u_ref[z * rows : (z + 1) * rows, :] = u
        acc_r = force if z == 0 else acc_r + force
        acc_ru = force * u if z == 0 else acc_ru + force * u
    top_ref[...] = u
    part_ref[:rows, :] = acc_r
    part_ref[rows:, :] = sum(acc_ru[m * srcs : (m + 1) * srcs] for m in range(comps))


def corner_of(index):
    return (index // 2 % 2) * 4 + (index // 4) * 2 + index % 2


def prepare_kernel(
    comps, srcs, n_slab, n_depth, cap, k_ref, top_ref, los_ref, map_ref, kh_ref, kl_ref, g_ref, pack_ref, y_ref
):
    size = 8 * comps
    full = size * srcs
    k_high, k_low = split2(k_ref[...])
    group = iota((full, size), 0) // srcs
    spread = onehot(corner_of(group // comps) * comps + group % comps == iota((full, size), 1)).astype(BF16)
    same = iota((full, full), 0) % srcs == iota((full, full), 1) % srcs
    for part, out in ((k_high, kh_ref), (k_low, kl_ref)):
        wide = dot_b(spread, part).astype(BF16)
        out[...] = jnp.where(same, dot_bt(wide, spread), 0.0).astype(BF16)
    block = comps * n_slab
    col = iota((block, size), 1)
    row_m = iota((block, size), 0) % comps
    corner = col // comps
    own = iota((block, block), 0) // comps
    other = iota((block, block), 1) // comps
    for v in range(4):
        keep = (col % comps == row_m) & ((corner // 2 % 2 == 1) | (v // 2 == 0))
        keep = keep & ((corner % 2 == 1) | (v % 2 == 0))
        low = onehot(keep & (corner // 4 == 0))
        high = onehot(keep & (corner // 4 == 1))
        k_lo, k_hi = dot(low, k_ref[...]), dot(high, k_ref[...])
        g_ref[2 * v * block : (2 * v + 1) * block, :] = jnp.where(
            other == own, dot_t(k_hi, high), jnp.where(other == own - 1, dot_t(k_hi, low), 0.0)
        )
        g_ref[(2 * v + 1) * block : (2 * v + 2) * block, :] = jnp.where(
            other == own, dot_t(k_lo, low), jnp.where(other == own + 1, dot_t(k_lo, high), 0.0)
        )
    nodes = map_ref.shape[1]
    tile = map_ref[...] // PIX
    per_row = srcs // n_depth
    los = los_ref[...]
    value = sum(los[m : m + 1, :] * top_ref[m * srcs : (m + 1) * srcs, :] for m in range(comps))
    y_ref[...] = jnp.zeros(y_ref.shape, F32)
    y_ref[:srcs, :] = value
    y_ref[srcs : srcs + comps, :] = los
    y_ref[srcs + comps : srcs + comps + 1, :] = (map_ref[...] % PIX).astype(F32)
    n_rows = 4 * n_depth
    row = iota((n_rows, y_ref.shape[0]), 0)
    pick = iota((n_rows, y_ref.shape[0]), 1)
    kind = row % 4
    first = jnp.where(kind == 1, row // 4 * per_row, jnp.where(kind == 2, srcs, srcs + 2))
    wide = jnp.concatenate(
        [dot(onehot((pick == first + a) & (kind > 0)), y_ref[...]) for a in range(2)], 1
    )
    parts = jnp.concatenate(split3(wide), 0)
    owner = onehot(iota((max(n_slab, 8), nodes), 0) == tile)
    before = onehot(iota((nodes, nodes), 0) < iota((nodes, nodes), 1)).astype(BF16)
    rank = jnp.sum(dot_b(owner.astype(BF16), before) * owner, 0, keepdims=True).astype(jnp.int32)
    lane = iota((LANES, nodes), 0)

    def one_tile(t, carry):
        here = jnp.where(tile == t, rank, -LANES)
        match = jnp.concatenate([onehot(lane == here), onehot(lane == here + cap)], 1).astype(BF16)
        got = dot_bt(parts, match)
        pack_ref[pl.ds(pl.multiple_of(t * n_rows, n_rows), n_rows), :] = (
            got[:n_rows] + got[n_rows : 2 * n_rows] + got[2 * n_rows :]
        )
        return carry

    lax.fori_loop(0, n_slab, one_tile, 0, unroll=n_slab <= 8)


def element_kernel(
    comps,
    srcs,
    wz,
    rank_ref,
    moduli_ref,
    material_ref,
    own_ref,
    left_ref,
    below_ref,
    corner_ref,
    part_ref,
    kh_ref,
    kl_ref,
    pack_ref,
    acc_ref,
    side_ref,
    down_ref,
    diag_ref,
    send_ref,
    uf_ref,
    uh_ref,
    ul_ref,
    z_ref,
):
    rows = comps * srcs
    width = own_ref.shape[1]
    lane = iota((rows, width), 1)
    inner = rank_ref[1] > 0
    material = material_ref[...]
    modulus = jnp.zeros(material.shape, F32)
    for level in range(moduli_ref.shape[0]):
        modulus = jnp.where(material == level, moduli_ref[level], modulus)
    side_ref[wz * rows :, :] = modulus
    down_ref[rows:, :] = modulus
    diag_ref[rows:, :] = modulus
    for z in range(-1, wz):
        for x in range(2):
            if z < 0:
                u = (corner_ref, below_ref)[x][...]
            else:
                u = (left_ref, own_ref)[x][z * rows : (z + 1) * rows, :]
            for y, value in enumerate((prev_lane(u, lane), u)):
                at = (((z + 1) * 2 + x) * 2 + y) * rows
                high, low = split2(value)
                uf_ref[at : at + rows, :] = value
                uh_ref[at : at + rows, :] = high
                ul_ref[at : at + rows, :] = low
    k_high, k_low = kh_ref[...], kl_ref[...]
    full = 8 * rows
    energy = jnp.zeros((rows, width), F32)
    sums = [jnp.zeros((rows, width), F32), jnp.zeros((rows, width), F32)]
    outs = (side_ref, acc_ref)
    edge = (diag_ref, down_ref)
    held = [None, None]
    for k in range(wz):
        at = k * 4 * rows
        u_high = uh_ref[at : at + full, :]
        force = dot_b(k_high, u_high) + dot_b(k_high, ul_ref[at : at + full, :]) + dot_b(k_low, u_high)
        force = force * modulus[k : k + 1, :]
        for c in range(8):
            energy = energy + force[c * rows : (c + 1) * rows] * uf_ref[at + c * rows : at + (c + 1) * rows, :]
        for x in range(2):
            def at_nodes(z):
                c = (z * 2 + x) * 2
                return force[(c + 1) * rows : (c + 2) * rows] + next_lane(force[c * rows : (c + 1) * rows], lane)

            lower, upper = at_nodes(0), at_nodes(1)
            if k == 0:
                edge[x][:rows, :] = lower
                sums[x] = sums[x] + jnp.where(inner, lower, 0.0) + upper
            else:
                outs[x][(k - 1) * rows : k * rows, :] = held[x] + lower
                sums[x] = sums[x] + lower + upper
            held[x] = upper
    for x in range(2):
        outs[x][(wz - 1) * rows : wz * rows, :] = held[x]
    z_ref[...] = jnp.zeros(z_ref.shape, F32)
    z_ref[:AT_DEN, :] = part_ref[...]
    z_ref[AT_DEN:AT_LOW, :] = sum(energy[m * srcs : (m + 1) * srcs] for m in range(comps))
    z_ref[AT_LOW : AT_LOW + rows, :] = sums[0]
    z_ref[AT_OWN : AT_OWN + rows, :] = sums[1]
    zrow = iota(modulus.shape, 0)
    bad = (zrow == 0) & jnp.logical_not(inner)
    good_sum = jnp.sum(jnp.where(bad, 0.0, modulus), 0, keepdims=True)
    bad_sum = jnp.sum(jnp.where(bad, modulus, 0.0), 0, keepdims=True)
    pick = jnp.where(iota((8, width), 0) // 2 == 0, good_sum, bad_sum)
    at_start = iota((8, width), 1) == 0
    pick = jnp.where(at_start == (iota((8, width), 0) % 2 == 1), pick, 0.0)
    z_ref[AT_MOD : AT_MOD + 8, :] = jnp.where(iota((8, width), 0) < 4, pick, 0.0)
    total = dot_t(jnp.ones((8, width), F32), z_ref[...])
    pack = pack_ref[...]
    send_ref[...] = jnp.where(
        iota(pack.shape, 0) % 4 == 0, jnp.broadcast_to(total[:1], pack.shape), pack
    )


def finish_kernel(
    comps,
    srcs,
    wz,
    n_slab,
    n_depth,
    cap,
    agg,
    rank_ref,
    got_ref,
    r_ref,
    acc_ref,
    mod_ref,
    side_ref,
    down_ref,
    diag_ref,
    kh_ref,
    kl_ref,
    g_ref,
    ci_ref,
    res_ref,
    pix_ref,
    c_ref,
    *halves,
):
    rows = comps * srcs
    width = r_ref.shape[1]
    n_dev = n_slab * n_depth
    block = comps * n_slab
    slab = rank_ref[0]
    depth = rank_ref[1]
    parts = got_ref[pl.ds(0, n_dev, stride=4), :]
    from_dev = iota((block, n_dev), 1) // n_depth
    to_slab = iota((block, n_dev), 0) // comps
    here = dot(onehot(from_dev == to_slab), parts)
    after = dot(onehot(from_dev == to_slab + 1), parts)
    total = dot(jnp.ones((8, n_dev), F32), parts)
    lane = iota((block, LANES), 1)
    comp = iota((block, LANES), 0) % comps
    lane8 = iota((8, LANES), 1)

    def own_lanes(start):
        return (lane >= start + comp * srcs) & (lane < start + (comp + 1) * srcs)

    stacked = jnp.concatenate(
        [
            jnp.where(own_lanes(0), here, 0.0),
            jnp.where(own_lanes(AT_OWN), here, 0.0) + jnp.where(own_lanes(AT_LOW), after, 0.0),
            jnp.where((lane8 >= AT_NUM) & (lane8 < AT_NUM + srcs), total, 0.0),
            jnp.where((lane8 >= AT_DEN) & (lane8 < AT_DEN + srcs), total, 0.0),
        ],
        0,
    )
    fold = onehot(iota((LANES, srcs), 0) % srcs == iota((LANES, srcs), 1))
    folded = dot(stacked, fold)
    sums = folded[:block]
    linear = folded[block : 2 * block]
    num = folded[2 * block : 2 * block + 1]
    den = folded[2 * block + 8 : 2 * block + 9]
    coarse = jnp.zeros((block, block), F32)
    for v in range(4):
        at = AT_MOD + v
        coarse = coarse + here[:, at : at + 1] * g_ref[2 * v * block : (2 * v + 1) * block, :]
        coarse = coarse + after[:, at : at + 1] * g_ref[(2 * v + 1) * block : (2 * v + 2) * block, :]
    corr = dot(ci_ref[...], sums / agg)
    num = num + jnp.sum(corr * sums, 0, keepdims=True)
    den = den + jnp.sum(corr * (2.0 * linear + dot(coarse, corr)), 0, keepdims=True)
    step = num / den
    step_col = jnp.sum(
        jnp.where(
            iota((rows, srcs), 0) % srcs == iota((rows, srcs), 1), jnp.broadcast_to(step, (rows, srcs)), 0.0
        ),
        1,
        keepdims=True,
    )
    which = iota((3 * rows, block), 0)
    source = iota((3 * rows, block), 1)
    near = onehot(
        (source % comps == which % rows // srcs) & (source // comps == slab - 1 + which // rows)
    )
    near = dot(near, corr)
    near = jnp.sum(
        jnp.where(iota((3 * rows, srcs), 0) % srcs == iota((3 * rows, srcs), 1), near, 0.0), 1, keepdims=True
    )
    full = 8 * rows
    stack = []
    for e in range(2):
        pieces = [near[(e + c // 2 % 2) * rows : (e + c // 2 % 2 + 1) * rows] for c in range(8)]
        stack.append(jnp.broadcast_to(jnp.concatenate(pieces, 0), (full, LANES)))
    lane_f = iota((full, LANES), 1)
    corner = iota((full, LANES), 0) // rows
    field = jnp.where(lane_f // 4 == 0, stack[0], jnp.where(lane_f // 4 == 1, stack[1], 0.0))
    field = jnp.where((corner // 4 == 0) & (lane_f // 2 % 2 == 1), 0.0, field)
    field = jnp.where((corner % 2 == 0) & (lane_f % 2 == 1), 0.0, field)
    f_high, f_low = split2(field)
    k_high = kh_ref[...]
    q = dot_b(k_high, f_high) + dot_b(k_high, f_low) + dot_b(kl_ref[...], f_high)
    at_start = iota((rows, width), 1) == 0

    def coefficient(e, z, y, edge):
        at = ((z * 2 + 1 - e) * 2 + y) * rows
        piece = q[at : at + rows]
        value = jnp.broadcast_to(piece[:, e * 4 + edge : e * 4 + edge + 1], (rows, width))
        if y == 1:
            other = jnp.broadcast_to(piece[:, e * 4 + edge + 1 : e * 4 + edge + 2], (rows, width))
            value = jnp.where(at_start, other, value)
        return value

    base = {(e, z, y): coefficient(e, z, y, 0) for e in range(2) for z in range(2) for y in range(2)}
    first = dict(base)
    for e in range(2):
        for y in range(2):
            first[e, 1, y] = jnp.where(depth == 0, coefficient(e, 1, y, 2), base[e, 1, y])
    mods = {}
    lane_m = iota((8, width), 1)
    for e in range(2):
        main = (mod_ref[rows:, :], side_ref[wz * rows :, :])[e]
        edge = (down_ref, diag_ref)[e][rows:, :]
        for y in range(2):
            a, b = (main, edge) if y == 1 else (next_lane(main, lane_m), next_lane(edge, lane_m))
            mods[e, y] = [a[k : k + 1, :] for k in range(wz)] + [b[:1, :]]
    to_halves(r_ref, halves)
    for z in range(wz):
        applied = acc_ref[z * rows : (z + 1) * rows, :] + side_ref[z * rows : (z + 1) * rows, :]
        if z == wz - 1:
            applied = applied + down_ref[:rows, :] + diag_ref[:rows, :]
        table = first if z == 0 else base
        for (e, up, y), value in table.items():
            applied = applied + value * mods[e, y][z + 1 - up]
        change = step_col * applied
        for h, half in enumerate(halves):
            at = pl.ds(z, rows, stride=wz)
            half[at, :] = half[at, :] - change[:, h * LANES : (h + 1) * LANES]
    for h, half in enumerate(halves):
        res_ref[:, h * LANES : (h + 1) * LANES] = half[...]
    per_row = srcs // n_depth
    slots = [got_ref[pl.ds((n_depth - 1) * 4 + j, n_slab, stride=4 * n_depth), :] for j in range(1, 4)]
    lane_s = iota((n_slab, LANES), 1)
    head = lane_s < cap

    def head_twice(x):
        return jnp.where(head, x, pltpu.roll(x, cap, 1))

    def tail_twice(x):
        return jnp.where(head, pltpu.roll(x, LANES - cap, 1), x)

    sight = (head_twice(slots[1]), tail_twice(slots[1]), head_twice(slots[2]))
    ids = tail_twice(slots[2])
    lane_e = iota((srcs, LANES), 1)
    mine = onehot(
        (iota((srcs, LANES), 0) == depth * per_row + lane_e // cap) & (lane_e < per_row * cap)
    )
    c_ref[...] = dot(corr, mine)
    value = slots[0]
    for m in range(comps):
        value = value + sight[m] * c_ref[pl.ds(m, n_slab, stride=comps), :]
    value = value * dot(jnp.broadcast_to(step, (8, srcs)), mine)[:1]
    value = jnp.where(lane_s < per_row * cap, value, 0.0)
    binned = jnp.zeros((24, PIX), F32)
    row8 = iota((8, LANES), 0)
    half = iota((8, LANES), 1) // cap
    pixel = iota((PIX, LANES), 0).astype(F32)
    for s in range(n_slab):
        vals = jnp.where(row8 == half, jnp.broadcast_to(value[s : s + 1], (8, LANES)), 0.0)
        match = onehot(pixel == ids[s : s + 1]).astype(BF16)
        binned = binned + dot_bt(jnp.concatenate(split3(vals), 0), match)
    binned = binned[:8] + binned[8:16] + binned[16:]
    pix_ref[...] = binned[:per_row]


def call(kernel, outs, scratch=(), name=None):
    def run(*args):
        specs = [
            pl.BlockSpec(memory_space=pltpu.SMEM if a.ndim == 1 else pltpu.VMEM) for a in args
        ]
        return pl.pallas_call(
            kernel,
            out_shape=[jax.ShapeDtypeStruct(s, d) for s, d in outs],
            in_specs=specs,
            out_specs=[pl.BlockSpec(memory_space=pltpu.VMEM)] * len(outs),
            scratch_shapes=[pltpu.VMEM(s, d) for s, d in scratch],
            name=name,
        )(*args)

    return run


def bind(kernel, *static):
    def run(*refs):
        kernel(*static, *refs)

    return run


def body(
    right_side,
    smoother,
    material,
    moduli,
    element_matrix,
    coarse_inverse,
    surface_map,
    line_of_sight,
):
    comps, srcs, width_x, wz, wy = right_side.shape
    n_slab = lax.axis_size("slab")
    n_depth = lax.axis_size("depth")
    if width_x != 1 or srcs != 8 or comps != 3 or wz != 8 or srcs // n_depth != 2:
        raise ValueError("unsupported shape")
    rows = comps * srcs
    n_dev = n_slab * n_depth
    block = comps * n_slab
    cap = 2 * width_x * wy // n_slab
    agg = float(width_x * wz * n_depth * wy)
    ranks = jnp.stack([lax.axis_index("slab"), lax.axis_index("depth")]).astype(jnp.int32)
    force = right_side.reshape(rows * wz, wy)

    up = [(s * n_depth + d, (s + 1) * n_depth + d + 1) for s in range(n_slab - 1) for d in range(n_depth - 1)]
    down = [(b, a) for a, b in up]
    slab_up = [(i, i + 1) for i in range(n_slab - 1)]
    slab_down = [(b, a) for a, b in slab_up]
    depth_up = [(i, i + 1) for i in range(n_depth - 1)]
    depth_down = [(b, a) for a, b in depth_up]
    both = ("slab", "depth")

    u, top, part = call(
        bind(weigh_kernel, comps, srcs, wz),
        [((wz * rows, wy), F32), ((rows, wy), F32), ((rows + srcs, wy), F32)],
        [((rows * wz, LANES), F32)] * (wy // LANES),
        name="weigh",
    )(force, smoother.reshape(comps * wz, wy))
    below = lax.ppermute(top, "depth", depth_up)
    corner = lax.ppermute(top, both, up)
    left = lax.ppermute(u, "slab", slab_up)
    k_high, k_low, g_parts, pack = call(
        bind(prepare_kernel, comps, srcs, n_slab, n_depth, cap),
        [
            ((8 * rows, 8 * rows), BF16),
            ((8 * rows, 8 * rows), BF16),
            ((8 * block, block), F32),
            ((4 * n_dev, LANES), F32),
        ],
        [((16, wy), F32)],
        name="prepare",
    )(element_matrix, top, line_of_sight.reshape(comps, wy), surface_map.reshape(1, wy))
    acc, side, below_force, diag, send = call(
        bind(element_kernel, comps, srcs, wz),
        [
            ((wz * rows, wy), F32),
            ((wz * rows + 8, wy), F32),
            ((rows + 8, wy), F32),
            ((rows + 8, wy), F32),
            ((4 * n_dev, LANES), F32),
        ],
        [
            ((4 * (wz + 1) * rows, wy), F32),
            ((4 * (wz + 1) * rows, wy), BF16),
            ((4 * (wz + 1) * rows, wy), BF16),
            ((LANES, wy), F32),
        ],
        name="elements",
    )(ranks, moduli, material.reshape(wz, wy), u, left, below, corner, part, k_high, k_low, pack)
    got = lax.all_to_all(send.reshape(n_dev, 4, LANES), both, 0, 0, tiled=True)
    side_got = lax.ppermute(side, "slab", slab_down)
    down_got = lax.ppermute(below_force, "depth", depth_down)
    diag_got = lax.ppermute(diag, both, down)
    residual, pixels = call(
        bind(finish_kernel, comps, srcs, wz, n_slab, n_depth, cap, agg),
        [((rows * wz, wy), F32), ((srcs // n_depth, PIX), F32)],
        [((block, LANES), F32)] + [((rows * wz, LANES), F32)] * (wy // LANES),
        name="finish",
    )(
        ranks,
        got.reshape(4 * n_dev, LANES),
        force,
        acc,
        below_force,
        side_got,
        down_got,
        diag_got,
        k_high,
        k_low,
        g_parts,
        coarse_inverse,
    )
    return (residual.reshape(right_side.shape), pixels)


def solution(mesh):
    return jax.shard_map(
        body,
        mesh=mesh,
        in_specs=(
            P(None, None, "slab", "depth", None),
            P(None, "slab", "depth", None),
            P("slab", "depth", None),
            P(),
            P(),
            P(),
            P("slab", None),
            P(None, "slab", None),
        ),
        out_specs=(P(None, None, "slab", "depth", None), P("depth", "slab")),
        check_vma=False,
    )
```
